256 devices in a mesh: shot: 64 (over x, y_lo, z), freq: 4 (over y_hi, core).
Axes of the slice: x: 4, y: 4 (y_hi: 2, y_lo: 2; y = y_hi * 2 + y_lo), z: 8, core: 2. Of those that a mesh axis runs over, the one named last changes fastest.
Arguments:
- data: bfloat16 [4, 2, 8192, 8192], P('freq', None, 'shot'), may hold values from -6 to 6
- primaries: bfloat16 [4, 2, 8192, 640], P('freq', None, 'shot'), may hold values from -0.15625 to 0.15625
- wavelet: float32 [4, 2], P('freq'), may hold values from 2 to 8
- cover_ids: int32 [8192, 8], P('shot'), may hold values from 0 to 15, all different within a row
- cover_counts: int32 [8192], P('shot'), may hold values from 1 to 8
Outputs:
- misfit: bfloat16 [4, 2, 8192, 8192], P('freq', None, 'shot')
- grad_primaries: float32 [4, 2, 8192, 640], P('freq', None, 'shot')
- wavelet_grad: float32 [128], replicated
The draws below stay inside these ranges and needn't reach their ends.
Inputs may be any that keep to these rules, and one draw needn't show every extreme that they name: `cover_ids`: the entries of a shot's list are different coverage blocks.
All inputs are finite; a program needn't handle non-finite values.
Results may differ from the reference program's by a relative error of at most 0.0013.
Values may be sent and summed in bfloat16 or wider, within the bound.
A program may use at most 128 MiB of HBM per device.

```python
import math
import jax
import jax.numpy as jnp
from jax import lax

NR = 8192
SD = 128
REACH = 2
RB = 512
CMAX = 8
NT = 128
NS = 8192
NF = 4
BAND = 640
STRIDE = 1
NRB = 16


def with_ends(result, stream_key, smallest, largest):
    shape = result.shape
    spot = [jax.random.randint(jax.random.fold_in(stream_key, axis), (), 0, shape[axis]) for axis in range(len(shape))]
    result = result.at[tuple(spot)].set(smallest)
    longest = shape.index(max(shape))
    spot[longest] = (spot[longest] + 1) % shape[longest]
    return result.at[tuple(spot)].set(largest)


def block_scale(stream_key, shape, shards, low, high):
    factor_of, own = 1.0, jax.random.fold_in(stream_key, 6)
    for axis_at, shards_of in shards:
        draws = jnp.exp(jax.random.uniform(jax.random.fold_in(own, axis_at), (shards_of,), jnp.float32, low / len(shards), high / len(shards)))
        factor_of = factor_of * jnp.repeat(draws, shape[axis_at] // shards_of).reshape([-1 if axis == axis_at else 1 for axis in range(len(shape))])
    return factor_of


def picks_of(key, rows, count, top, lift):
    sequence = jax.random.permutation(jax.random.fold_in(key, 1), count)
    boost = sequence
    for power in range(3):
        boost = boost * boost // count
    boost = boost * lift // count
    chance = jax.random.randint(jax.random.fold_in(key, 2), (rows, count), 0, 4096) + boost
    sure = jax.random.permutation(jax.random.fold_in(key, 3), rows)[jnp.arange(count) % rows]
    chance = jnp.where(jnp.arange(rows)[:, None] == sure[None, :], 1 << 14, chance)
    score = chance * count + jnp.arange(count)
    return lax.top_k(score.astype(jnp.int32), top)[1].astype(jnp.int32)


def centred(own_key, shape, width, bound, cuts=(), held_as=jnp.bfloat16):
    array = jax.random.normal(own_key, shape, jnp.float32) * width
    if len(cuts) > 0:
        array = block_scale(own_key, shape, cuts, -0.22, 0.18) * array
    return jnp.clip(array, min=-bound, max=bound).astype(held_as)


def setup_inputs(seed: int = 0) -> dict:
    arg_keys = jax.random.split(jax.random.key(seed), 6)
    data = centred(arg_keys[0], (NF, 2, NS, NR), 1.0, 6.0, ((0, 4), (2, 64)))
    primaries = centred(arg_keys[1], (NF, 2, NS, BAND), (2 * BAND) ** -0.5, 0.15625, ((0, 4), (2, 64)))
    wavelet = jnp.clip(2.0 + 6.0 * jax.random.uniform(arg_keys[2], (NF, 2), jnp.float32) ** block_scale(arg_keys[2], (NF, 2), ((0, 4),), -0.2, 0.2), 2.0, 8.0)
    cover_ids = picks_of(arg_keys[3], NS, NRB, CMAX, 4096)
    cover_counts = with_ends(jax.random.randint(arg_keys[4], (NS,), 1, CMAX + 1), jax.random.fold_in(arg_keys[4], 1), 1, CMAX).astype(jnp.int32)
    return dict(data=data, primaries=primaries, wavelet=wavelet, cover_ids=cover_ids, cover_counts=cover_counts)


def reference(data, primaries, wavelet, cover_ids, cover_counts):
    block_count = NS // SD
    block_ids = jnp.arange(NRB, dtype=jnp.int32)
    listed = jnp.arange(CMAX, dtype=jnp.int32)[None, :] < cover_counts[:, None]
    covered = jnp.any((cover_ids[:, :, None] == block_ids[None, None, :]) & listed[:, :, None], axis=1).astype(jnp.float32)
    columns = jnp.arange(NR, dtype=jnp.int32)
    highest = lax.Precision.HIGHEST
    misfits = []
    gradients = []
    correlations = []
    for freq_index in range(NF):
        rows_padded = jnp.pad(data[freq_index], ((0, 0), (REACH * SD, REACH * SD), (0, 0)))
        wave_re = wavelet[freq_index, 0]
        wave_im = wavelet[freq_index, 1]
        response_all = primaries[freq_index]
        record_all = data[freq_index]

        def one_block(block):
            start = (block * SD).astype(jnp.int32)
            nearby = lax.dynamic_slice(rows_padded, (jnp.int32(0), start, jnp.int32(0)), (2, BAND, NR)).astype(jnp.float32)
            shot_ids = start - REACH * SD + jnp.arange(BAND, dtype=jnp.int32)
            direct_hit = columns[None, :] == shot_ids[:, None] * STRIDE
            operand = jnp.stack([jnp.where(direct_hit, wave_re, 0.0) - nearby[0], jnp.where(direct_hit, wave_im, 0.0) - nearby[1]])
            operand = lax.optimization_barrier(operand.astype(jnp.bfloat16)).astype(jnp.float32)
            response = lax.dynamic_slice(response_all, (jnp.int32(0), start, jnp.int32(0)), (2, SD, BAND)).astype(jnp.float32)
            pred_re = jnp.dot(response[0], operand[0], precision=highest) - jnp.dot(response[1], operand[1], precision=highest)
            pred_im = jnp.dot(response[0], operand[1], precision=highest) + jnp.dot(response[1], operand[0], precision=highest)
            record = lax.dynamic_slice(record_all, (jnp.int32(0), start, jnp.int32(0)), (2, SD, NR)).astype(jnp.float32)
            mask = jnp.repeat(lax.dynamic_slice(covered, (start, jnp.int32(0)), (SD, NRB)), RB, axis=1)
            misfit = (mask[None] * (record - jnp.stack([pred_re, pred_im]))).astype(jnp.bfloat16)
            resid = lax.optimization_barrier(misfit).astype(jnp.float32)
            grad_re = -(jnp.dot(resid[0], operand[0].T, precision=highest) + jnp.dot(resid[1], operand[1].T, precision=highest))
            grad_im = -(jnp.dot(resid[1], operand[0].T, precision=highest) - jnp.dot(resid[0], operand[1].T, precision=highest))
            sources = jnp.pad(resid[:, :, ::STRIDE], ((0, 0), (0, 0), (REACH * SD, REACH * SD)))
            sources = lax.dynamic_slice(sources, (jnp.int32(0), jnp.int32(0), start), (2, SD, BAND))
            corr_re = -jnp.sum(response[0] * sources[0] + response[1] * sources[1])
            corr_im = -jnp.sum(response[0] * sources[1] - response[1] * sources[0])
            return (misfit, jnp.stack([grad_re, grad_im]), jnp.stack([corr_re, corr_im]))
        errs, grads, corr = lax.map(one_block, jnp.arange(block_count, dtype=jnp.int32))
        misfits.append(jnp.transpose(errs, (1, 0, 2, 3)).reshape(2, NS, NR))
        gradients.append(jnp.transpose(grads, (1, 0, 2, 3)).reshape(2, NS, BAND))
        correlations.append(lax.optimization_barrier(jnp.sum(corr, axis=0)))
    times = jnp.arange(NT, dtype=jnp.int32).astype(jnp.float32)
    series = jnp.zeros((NT,), jnp.float32)
    for freq_index in range(NF):
        phase = 2.0 * math.pi * (freq_index + 1) * times / NT
        series = series + correlations[freq_index][0] * jnp.cos(phase) - correlations[freq_index][1] * jnp.sin(phase)
    wavelet_grad = series / math.sqrt(NS * BAND)
    return (jnp.stack(misfits), jnp.stack(gradients), wavelet_grad)
```

```python
import functools
import math

import jax
import jax.numpy as jnp
import numpy as np
from jax import lax
from jax.experimental import pallas as pl
from jax.experimental.pallas import tpu as pltpu
from jax.sharding import PartitionSpec as P

RB = 512
NT = 128
REACH = 2
PRE = 3
LAG = 4
RADIX = 4
MESH = pl.DeviceIdType.MESH


def kernel(
    dims,
    data,
    prim,
    wave,
    ids,
    counts,
    waves,
    misfit,
    grad,
    wavelet_grad,
    rec,
    own,
    near,
    mix,
    outer,
    stage,
    window,
    sums,
    own_sem,
    rec_sem,
    out_sem,
    send_sem,
    recv_sem,
    sum_send_sem,
    sum_recv_sem,
):
    shots, freqs, chunks, rows = dims
    width = own.shape[3]
    tiles = width // rows
    me = lax.axis_index("shot")
    freq = lax.axis_index("freq")
    right = lax.rem(me + 1, shots)
    left = lax.rem(me + shots - 1, shots)

    def first_of(block):
        return lax.rem(lax.div(block, tiles) + chunks - 1, chunks)

    own_first = first_of(me)
    left_first = first_of(left)
    right_first = first_of(right)
    work_first = lax.rem(lax.div(me + shots - REACH, tiles), chunks)

    def load_own(chunk):
        columns = pl.ds(pl.multiple_of(chunk * width, width), width)
        return pltpu.make_async_copy(
            data.at[0, :, :, columns], own.at[chunk], own_sem.at[chunk]
        )

    load_rec = pltpu.make_async_copy(data.at[0], rec, rec_sem.at[0])

    def hop(stream, chunk):
        src = own.at[chunk] if stream < 2 else near.at[stream - 2, chunk]
        target = right if stream % 2 == 0 else left
        return pltpu.make_async_remote_copy(
            src_ref=src,
            dst_ref=near.at[stream, chunk],
            send_sem=send_sem.at[stream, chunk],
            recv_sem=recv_sem.at[stream, chunk],
            device_id=(target, freq),
            device_id_type=MESH,
        )

    digits = [freq, lax.rem(me, 4), lax.rem(lax.div(me, 4), 4), lax.div(me, 16)]

    def partner(level, digit):
        if level == 0:
            return (me, digit)
        scale = (1, 4, 16)[level - 1]
        return (me + (digit - digits[level]) * scale, freq)

    def exchange(level, step):
        digit = lax.rem(digits[level] + step, RADIX)
        return pltpu.make_async_remote_copy(
            src_ref=sums.at[level, digits[level]],
            dst_ref=sums.at[level, digits[level]],
            send_sem=sum_send_sem.at[level, step - 1],
            recv_sem=sum_recv_sem.at[level, digits[level]],
            device_id=partner(level, digit),
            device_id_type=MESH,
        )

    def arrival(level, step):
        digit = lax.rem(digits[level] + step, RADIX)
        return pltpu.make_async_remote_copy(
            src_ref=sums.at[level, digit],
            dst_ref=sums.at[level, digit],
            send_sem=sum_send_sem.at[level, step - 1],
            recv_sem=sum_recv_sem.at[level, digit],
            device_id=partner(level, digit),
            device_id_type=MESH,
        )

    def sum_send(level, value):
        sums[level, digits[level]] = value
        for step in range(1, RADIX):
            exchange(level, step).start()

    def sum_take(level):
        for step in range(1, RADIX):
            arrival(level, step).wait_recv()
        total = sums[level, 0]
        for digit in range(1, RADIX):
            total = total + sums[level, digit]
        return total

    for step in range(chunks):
        load_own(lax.rem(own_first + step, chunks)).start()
    load_rec.start()

    barrier = pltpu.get_barrier_semaphore()
    for target in (left, right):
        pl.semaphore_signal(barrier, inc=1, device_id=(target, freq), device_id_type=MESH)
    for level in range(4):
        for step in range(1, RADIX):
            pl.semaphore_signal(
                barrier,
                inc=1,
                device_id=partner(level, lax.rem(digits[level] + step, RADIX)),
                device_id_type=MESH,
            )
    pl.semaphore_wait(barrier, 2 + 4 * (RADIX - 1))

    diagonal = lax.broadcasted_iota(jnp.int32, (rows, rows), 0) == lax.broadcasted_iota(
        jnp.int32, (rows, rows), 1
    )
    for step in range(PRE):
        chunk = lax.rem(own_first + step, chunks)
        load_own(chunk).wait()
        if step == 1:
            spot = pl.ds(pl.multiple_of(lax.rem(me, tiles) * rows, rows), rows)
            for part in range(2):
                tile = own[chunk, part, :, spot]
                moved = (tile.astype(jnp.float32) - wave[0, part]).astype(jnp.bfloat16)
                own[chunk, part, :, spot] = jnp.where(diagonal, moved, tile)
        for stream in range(2):
            hop(stream, chunk).start()

    def inside(block):
        there = me + block - REACH
        return jnp.where(jnp.logical_and(there >= 0, there < shots), 1.0, 0.0)

    def response(part, block):
        tile = prim[0, part, :, pl.ds(block * rows, rows)]
        return tile.astype(jnp.float32) * inside(block)

    for block in range(2 * REACH + 1):
        real = response(0, block)
        imag = response(1, block)
        mix[block, pl.ds(0, rows), pl.ds(0, rows)] = real.astype(jnp.bfloat16)
        mix[block, pl.ds(0, rows), pl.ds(rows, rows)] = (-imag).astype(jnp.bfloat16)
        mix[block, pl.ds(rows, rows), pl.ds(0, rows)] = imag.astype(jnp.bfloat16)
        mix[block, pl.ds(rows, rows), pl.ds(rows, rows)] = real.astype(jnp.bfloat16)
    outer[...] = jnp.zeros_like(outer)
    load_rec.wait()

    def rows_of(block, chunk):
        ref = own.at[chunk] if block == REACH else near.at[(2, 0, -1, 1, 3)[block], chunk]
        return ref[...].reshape(2 * rows, width)

    def out_copy(slot, chunk):
        columns = pl.ds(pl.multiple_of(chunk * width, width), width)
        return pltpu.make_async_copy(
            stage.at[slot], misfit.at[0, :, :, columns], out_sem.at[slot]
        )

    def work(step):
        chunk = lax.rem(work_first + step, chunks)
        slot = lax.rem(step, 2)
        for stream in (2, 3):
            hop(stream, chunk).wait_recv()
        columns = pl.ds(pl.multiple_of(chunk * width, width), width)
        predicted = jnp.dot(mix[0], rows_of(0, chunk), preferred_element_type=jnp.float32)
        for block in range(1, 2 * REACH + 1):
            predicted += jnp.dot(
                mix[block], rows_of(block, chunk), preferred_element_type=jnp.float32
            )
        entry = lax.broadcasted_iota(jnp.int32, ids.shape, 1)
        hit = jnp.logical_and(ids[...] == chunk, entry < counts[...])
        mask = jnp.sum(jnp.where(hit, 1.0, 0.0), axis=1, keepdims=True)
        record = rec[:, :, columns].astype(jnp.float32)
        residual = (mask[None] * (record + predicted.reshape(2, rows, width))).astype(
            jnp.bfloat16
        )

        @pl.when(step >= 2)
        def _():
            out_copy(slot, chunk).wait()

        stage[slot] = residual
        out_copy(slot, chunk).start()

        @pl.when(step < 2)
        def _():
            window[:, :, pl.ds(pl.multiple_of(step * width, width), width)] = residual

        flat = residual.reshape(2 * rows, width)
        for block in range(2 * REACH + 1):
            outer[block] += lax.dot_general(
                flat,
                rows_of(block, chunk),
                (((1,), (1,)), ((), ())),
                preferred_element_type=jnp.float32,
            )

    def correlate():
        offset = lax.rem(me + shots - REACH, tiles) * rows
        real = jnp.zeros((rows, rows), jnp.float32)
        imag = jnp.zeros((rows, rows), jnp.float32)
        for block in range(2 * REACH + 1):
            spot = pl.ds(pl.multiple_of(offset + block * rows, rows), rows)
            resid_re = window[0, :, spot].astype(jnp.float32)
            resid_im = window[1, :, spot].astype(jnp.float32)
            resp_re = response(0, block)
            resp_im = response(1, block)
            real += resp_re * resid_re + resp_im * resid_im
            imag += resp_re * resid_im - resp_im * resid_re
        line = lax.broadcasted_iota(jnp.int32, waves.shape, 0)
        cosine = jnp.sum(jnp.where(line == freq, waves[...], 0.0), axis=0, keepdims=True)
        sine = jnp.sum(jnp.where(line == freq + freqs, waves[...], 0.0), axis=0, keepdims=True)
        series = jnp.sum(imag) * sine - jnp.sum(real) * cosine
        return jnp.broadcast_to(series, sums.shape[2:])

    def body(step, carry):
        @pl.when(step < chunks)
        def _():
            chunk = lax.rem(left_first + step, chunks)
            hop(0, chunk).wait_recv()
            hop(2, chunk).start()
            chunk = lax.rem(right_first + step, chunks)
            hop(1, chunk).wait_recv()
            hop(3, chunk).start()

        @pl.when(step < chunks - PRE)
        def _():
            chunk = lax.rem(own_first + step + PRE, chunks)
            load_own(chunk).wait()
            for stream in range(2):
                hop(stream, chunk).start()

        @pl.when(step >= LAG)
        def _():
            work(step - LAG)

        @pl.when(step == LAG + 1)
        def _():
            sum_send(0, correlate())

        for level in range(4):

            @pl.when(step == LAG + 3 + 2 * level)
            def _(level=level):
                total = sum_take(level)
                if level < 3:
                    sum_send(level + 1, total)
                else:
                    scale = 1.0 / math.sqrt(shots * rows * rows * (2 * REACH + 1))
                    wavelet_grad[...] = total * scale

        return carry

    lax.fori_loop(0, chunks + LAG, body, 0)

    for block in range(2 * REACH + 1):
        spot = pl.ds(block * rows, rows)
        low, high = pl.ds(0, rows), pl.ds(rows, rows)
        real = outer[block, low, low] + outer[block, high, high]
        imag = outer[block, high, low] - outer[block, low, high]
        grad[0, 0, :, spot] = real * inside(block)
        grad[0, 1, :, spot] = imag * inside(block)

    for slot in range(2):
        out_copy(slot, 0).wait()
    for level in range(4):
        for step in range(1, RADIX):
            exchange(level, step).wait_send()

    def drain(chunk, carry):
        for stream in range(4):
            hop(stream, chunk).wait_send()
        return carry

    lax.fori_loop(0, chunks, drain, 0)


def on_device(shots, freqs, data, primaries, wavelet, cover_ids, cover_counts):
    _, _, rows, width = data.shape
    chunks = width // RB
    band = primaries.shape[3]
    times = np.arange(NT, dtype=np.float32)
    phase = np.stack(
        [np.float32(2.0 * math.pi * (f + 1)) * times / np.float32(NT) for f in range(freqs)]
    )
    waves = jnp.asarray(np.concatenate([np.cos(phase), np.sin(phase)]).astype(np.float32))
    vmem = pl.BlockSpec(memory_space=pltpu.VMEM)
    hbm = pl.BlockSpec(memory_space=pl.ANY)
    blocks = 2 * REACH + 1
    dma = pltpu.SemaphoreType.DMA
    misfit, grad, series = pl.pallas_call(
        functools.partial(kernel, (shots, freqs, chunks, rows)),
        out_shape=(
            jax.ShapeDtypeStruct(data.shape, jnp.bfloat16),
            jax.ShapeDtypeStruct((1, 2, rows, band), jnp.float32),
            jax.ShapeDtypeStruct((8, NT), jnp.float32),
        ),
        in_specs=[hbm, vmem, pl.BlockSpec(memory_space=pltpu.SMEM), vmem, vmem, vmem],
        out_specs=(hbm, vmem, vmem),
        scratch_shapes=[
            pltpu.VMEM((2, rows, width), jnp.bfloat16),
            pltpu.VMEM((chunks, 2, rows, RB), jnp.bfloat16),
            pltpu.VMEM((4, chunks, 2, rows, RB), jnp.bfloat16),
            pltpu.VMEM((blocks, 2 * rows, 2 * rows), jnp.bfloat16),
            pltpu.VMEM((blocks, 2 * rows, 2 * rows), jnp.float32),
            pltpu.VMEM((2, 2, rows, RB), jnp.bfloat16),
            pltpu.VMEM((2, rows, 2 * RB), jnp.bfloat16),
            pltpu.VMEM((4, RADIX, 8, NT), jnp.float32),
            dma((chunks,)),
            dma((1,)),
            dma((2,)),
            dma((4, chunks)),
            dma((4, chunks)),
            dma((4, RADIX - 1)),
            dma((4, RADIX)),
        ],
        compiler_params=pltpu.CompilerParams(
            collective_id=0, has_side_effects=True, vmem_limit_bytes=48 * 1024 * 1024
        ),
    )(data, primaries, wavelet, cover_ids, cover_counts.reshape(rows, 1), waves)
    return misfit, grad, series[0]


def solution(mesh):
    in_specs = (
        P("freq", None, "shot", None),
        P("freq", None, "shot", None),
        P("freq", None),
        P("shot", None),
        P("shot"),
    )
    out_specs = (P("freq", None, "shot", None), P("freq", None, "shot", None), P())
    return jax.shard_map(
        functools.partial(on_device, mesh.shape["shot"], mesh.shape["freq"]),
        mesh=mesh,
        in_specs=in_specs,
        out_specs=out_specs,
        check_vma=False,
    )
```

```python
import functools
import math

import jax
import jax.numpy as jnp
import numpy as np
from jax import lax
from jax.experimental import pallas as pl
from jax.experimental.pallas import tpu as pltpu
from jax.sharding import PartitionSpec as P

RB = 512
NT = 128
REACH = 2
PRE = 6
LAG = 5
TAKE = 11
RADIX = 16
LEVELS = 2
MESH = pl.DeviceIdType.MESH


def kernel(
    dims,
    data,
    prim_hbm,
    wave_hbm,
    ids_hbm,
    counts_hbm,
    waves_hbm,
    misfit,
    grad,
    wavelet_grad,
    rec,
    own,
    near,
    mix,
    outer,
    stage,
    window,
    sums,
    prim,
    wave,
    ids,
    counts,
    waves,
    cover,
    small_sem,
    own_sem,
    rec_sem,
    out_sem,
    send_sem,
    recv_sem,
    sum_send_sem,
    sum_recv_sem,
):
    shots, freqs, chunks, rows = dims
    width = own.shape[3]
    tiles = width // rows
    me = lax.axis_index("shot")
    freq = lax.axis_index("freq")
    right = lax.rem(me + 1, shots)
    left = lax.rem(me + shots - 1, shots)

    def first_of(block):
        return lax.rem(lax.div(block, tiles) + chunks - 1, chunks)

    own_first = first_of(me)
    left_first = first_of(left)
    right_first = first_of(right)
    work_first = lax.rem(lax.div(me + shots - REACH, tiles), chunks)

    def load_own(chunk):
        columns = pl.ds(pl.multiple_of(chunk * width, width), width)
        return pltpu.make_async_copy(
            data.at[0, :, :, columns], own.at[chunk], own_sem.at[chunk]
        )

    load_rec = pltpu.make_async_copy(data.at[0], rec, rec_sem.at[0])

    def hop(stream, chunk):
        src = own.at[chunk] if stream < 2 else near.at[stream - 2, chunk]
        target = right if stream % 2 == 0 else left
        return pltpu.make_async_remote_copy(
            src_ref=src,
            dst_ref=near.at[stream, chunk],
            send_sem=send_sem.at[stream, chunk],
            recv_sem=recv_sem.at[stream, chunk],
            device_id=(target, freq),
            device_id_type=MESH,
        )

    line = RADIX // 2
    digits = [
        lax.rem(freq, 2) * line + lax.rem(me, line),
        lax.div(freq, 2) * line + lax.div(me, line),
    ]

    def partner(level, digit):
        first, second = lax.rem(digit, line), lax.div(digit, line)
        if level == 0:
            return (me - lax.rem(me, line) + first, freq - lax.rem(freq, 2) + second)
        return (first * line + lax.rem(me, line), second * 2 + lax.rem(freq, 2))

    def exchange(level, step):
        digit = lax.rem(digits[level] + step, RADIX)
        return pltpu.make_async_remote_copy(
            src_ref=sums.at[level, digits[level]],
            dst_ref=sums.at[level, digits[level]],
            send_sem=sum_send_sem.at[level, step - 1],
            recv_sem=sum_recv_sem.at[level, digits[level]],
            device_id=partner(level, digit),
            device_id_type=MESH,
        )

    def arrival(level, step):
        digit = lax.rem(digits[level] + step, RADIX)
        return pltpu.make_async_remote_copy(
            src_ref=sums.at[level, digit],
            dst_ref=sums.at[level, digit],
            send_sem=sum_send_sem.at[level, step - 1],
            recv_sem=sum_recv_sem.at[level, digit],
            device_id=partner(level, digit),
            device_id_type=MESH,
        )

    def sum_send(level, value):
        sums[level, digits[level]] = value
        for step in range(1, RADIX):
            exchange(level, step).start()

    def sum_take(level):
        for step in range(1, RADIX):
            arrival(level, step).wait_recv()
        total = sums[level, 0]
        for digit in range(1, RADIX):
            total = total + sums[level, digit]
        return total

    for step in range(chunks):
        load_own(lax.rem(own_first + step, chunks)).start()
    small = [
        pltpu.make_async_copy(source, target, small_sem.at[spot])
        for spot, (source, target) in enumerate(
            [
                (wave_hbm, wave),
                (prim_hbm, prim),
                (ids_hbm, ids),
                (counts_hbm, counts),
                (waves_hbm, waves),
            ]
        )
    ]
    for copy in small:
        copy.start()
    load_rec.start()

    barrier = pltpu.get_barrier_semaphore()
    for target in (left, right):
        pl.semaphore_signal(barrier, inc=1, device_id=(target, freq), device_id_type=MESH)
    for level in range(LEVELS):
        for step in range(1, RADIX):
            pl.semaphore_signal(
                barrier,
                inc=1,
                device_id=partner(level, lax.rem(digits[level] + step, RADIX)),
                device_id_type=MESH,
            )
    pl.semaphore_wait(barrier, 2 + LEVELS * (RADIX - 1))

    small[0].wait()
    diagonal = lax.broadcasted_iota(jnp.int32, (rows, rows), 0) == lax.broadcasted_iota(
        jnp.int32, (rows, rows), 1
    )
    for step in range(PRE):
        chunk = lax.rem(own_first + step, chunks)
        load_own(chunk).wait()
        if step == 1:
            spot = pl.ds(pl.multiple_of(lax.rem(me, tiles) * rows, rows), rows)
            for part in range(2):
                tile = own[chunk, part, :, spot]
                moved = (tile.astype(jnp.float32) - wave[pl.ds(0, 1), pl.ds(part, 1)]).astype(jnp.bfloat16)
                own[chunk, part, :, spot] = jnp.where(diagonal, moved, tile)
        for stream in range(2):
            hop(stream, chunk).start()

    for copy in small[1:]:
        copy.wait()
    entry = lax.broadcasted_iota(jnp.int32, ids.shape, 0)
    listed = entry < counts[...]
    cover[...] = jnp.zeros_like(cover)
    for chunk in range(chunks):
        hit = jnp.logical_and(ids[...] == chunk, listed)
        cover[pl.ds(chunk, 1), :] = jnp.sum(jnp.where(hit, 1.0, 0.0), axis=0, keepdims=True)
    cover[...] = cover[...].T

    def inside(block):
        there = me + block - REACH
        return jnp.where(jnp.logical_and(there >= 0, there < shots), 1.0, 0.0)

    def response(part, block):
        tile = prim[0, part, :, pl.ds(block * rows, rows)]
        return tile.astype(jnp.float32) * inside(block)

    for block in range(2 * REACH + 1):
        real = response(0, block)
        imag = response(1, block)
        mix[block, pl.ds(0, rows), pl.ds(0, rows)] = real.astype(jnp.bfloat16)
        mix[block, pl.ds(0, rows), pl.ds(rows, rows)] = (-imag).astype(jnp.bfloat16)
        mix[block, pl.ds(rows, rows), pl.ds(0, rows)] = imag.astype(jnp.bfloat16)
        mix[block, pl.ds(rows, rows), pl.ds(rows, rows)] = real.astype(jnp.bfloat16)
    outer[...] = jnp.zeros_like(outer)
    load_rec.wait()

    def rows_of(block, chunk):
        ref = own.at[chunk] if block == REACH else near.at[(2, 0, -1, 1, 3)[block], chunk]
        return ref[...].reshape(2 * rows, width)

    def out_copy(slot, chunk):
        columns = pl.ds(pl.multiple_of(chunk * width, width), width)
        return pltpu.make_async_copy(
            stage.at[slot], misfit.at[0, :, :, columns], out_sem.at[slot]
        )

    def work(step):
        chunk = lax.rem(work_first + step, chunks)
        slot = lax.rem(step, 2)
        for stream in (2, 3):
            hop(stream, chunk).wait_recv()
        columns = pl.ds(pl.multiple_of(chunk * width, width), width)
        predicted = jnp.dot(mix[0], rows_of(0, chunk), preferred_element_type=jnp.float32)
        for block in range(1, 2 * REACH + 1):
            predicted += jnp.dot(
                mix[block], rows_of(block, chunk), preferred_element_type=jnp.float32
            )
        lane = lax.broadcasted_iota(jnp.int32, cover.shape, 1)
        mask = jnp.sum(jnp.where(lane == chunk, cover[...], 0.0), axis=1, keepdims=True)
        record = rec[:, :, columns].astype(jnp.float32)
        residual = (mask[None] * (record + predicted.reshape(2, rows, width))).astype(
            jnp.bfloat16
        )

        @pl.when(step >= 2)
        def _():
            out_copy(slot, chunk).wait()

        stage[slot] = residual
        out_copy(slot, chunk).start()

        @pl.when(step < 2)
        def _():
            window[:, :, pl.ds(pl.multiple_of(step * width, width), width)] = residual

        flat = residual.reshape(2 * rows, width)
        for block in range(2 * REACH + 1):
            outer[block] += lax.dot_general(
                flat,
                rows_of(block, chunk),
                (((1,), (1,)), ((), ())),
                preferred_element_type=jnp.float32,
            )

    def correlate():
        offset = lax.rem(me + shots - REACH, tiles) * rows
        real = jnp.zeros((rows, rows), jnp.float32)
        imag = jnp.zeros((rows, rows), jnp.float32)
        for block in range(2 * REACH + 1):
            spot = pl.ds(pl.multiple_of(offset + block * rows, rows), rows)
            resid_re = window[0, :, spot].astype(jnp.float32)
            resid_im = window[1, :, spot].astype(jnp.float32)
            resp_re = response(0, block)
            resp_im = response(1, block)
            real += resp_re * resid_re + resp_im * resid_im
            imag += resp_re * resid_im - resp_im * resid_re
        line = lax.broadcasted_iota(jnp.int32, waves.shape, 0)
        cosine = jnp.sum(jnp.where(line == freq, waves[...], 0.0), axis=0, keepdims=True)
        sine = jnp.sum(jnp.where(line == freq + freqs, waves[...], 0.0), axis=0, keepdims=True)
        series = jnp.sum(imag) * sine - jnp.sum(real) * cosine
        return jnp.broadcast_to(series, sums.shape[2:])

    def body(step, carry):
        @pl.when(step < chunks)
        def _():
            chunk = lax.rem(left_first + step, chunks)
            hop(0, chunk).wait_recv()
            hop(2, chunk).start()
            chunk = lax.rem(right_first + step, chunks)
            hop(1, chunk).wait_recv()
            hop(3, chunk).start()

        @pl.when(step < chunks - PRE)
        def _():
            chunk = lax.rem(own_first + step + PRE, chunks)
            load_own(chunk).wait()
            for stream in range(2):
                hop(stream, chunk).start()

        @pl.when(step >= LAG)
        def _():
            work(step - LAG)

        @pl.when(step == LAG + 1)
        def _():
            sum_send(0, correlate())

        @pl.when(step == TAKE)
        def _():
            sum_send(1, sum_take(0))

        return carry

    lax.fori_loop(0, chunks + LAG, body, 0)

    for block in range(2 * REACH + 1):
        spot = pl.ds(block * rows, rows)
        low, high = pl.ds(0, rows), pl.ds(rows, rows)
        real = outer[block, low, low] + outer[block, high, high]
        imag = outer[block, high, low] - outer[block, low, high]
        grad[0, 0, :, spot] = real * inside(block)
        grad[0, 1, :, spot] = imag * inside(block)

    scale = 1.0 / math.sqrt(shots * rows * rows * (2 * REACH + 1))
    wavelet_grad[...] = sum_take(1) * scale

    for slot in range(2):
        out_copy(slot, 0).wait()
    for level in range(LEVELS):
        for step in range(1, RADIX):
            exchange(level, step).wait_send()

    def drain(chunk, carry):
        for stream in range(4):
            hop(stream, chunk).wait_send()
        return carry

    lax.fori_loop(0, chunks, drain, 0)


def on_device(shots, freqs, data, primaries, wavelet, cover_ids, cover_counts):
    _, _, rows, width = data.shape
    chunks = width // RB
    band = primaries.shape[3]
    times = np.arange(NT, dtype=np.float32)
    phase = np.stack(
        [np.float32(2.0 * math.pi * (f + 1)) * times / np.float32(NT) for f in range(freqs)]
    )
    waves = jnp.asarray(np.concatenate([np.cos(phase), np.sin(phase)]).astype(np.float32))
    vmem = pl.BlockSpec(memory_space=pltpu.VMEM)
    hbm = pl.BlockSpec(memory_space=pltpu.HBM)
    blocks = 2 * REACH + 1
    dma = pltpu.SemaphoreType.DMA
    misfit, grad, series = pl.pallas_call(
        functools.partial(kernel, (shots, freqs, chunks, rows)),
        out_shape=(
            jax.ShapeDtypeStruct(data.shape, jnp.bfloat16),
            jax.ShapeDtypeStruct((1, 2, rows, band), jnp.float32),
            jax.ShapeDtypeStruct((1, NT), jnp.float32),
        ),
        in_specs=[hbm] * 6,
        out_specs=(pl.BlockSpec(memory_space=pl.ANY), vmem, vmem),
        scratch_shapes=[
            pltpu.VMEM((2, rows, width), jnp.bfloat16),
            pltpu.VMEM((chunks, 2, rows, RB), jnp.bfloat16),
            pltpu.VMEM((4, chunks, 2, rows, RB), jnp.bfloat16),
            pltpu.VMEM((blocks, 2 * rows, 2 * rows), jnp.bfloat16),
            pltpu.VMEM((blocks, 2 * rows, 2 * rows), jnp.float32),
            pltpu.VMEM((2, 2, rows, RB), jnp.bfloat16),
            pltpu.VMEM((2, rows, 2 * RB), jnp.bfloat16),
            pltpu.VMEM((LEVELS, RADIX, 1, NT), jnp.float32),
            pltpu.VMEM(primaries.shape, jnp.bfloat16),
            pltpu.VMEM(wavelet.shape, jnp.float32),
            pltpu.VMEM(cover_ids.shape[::-1], jnp.int32),
            pltpu.VMEM((1, rows), jnp.int32),
            pltpu.VMEM(waves.shape, jnp.float32),
            pltpu.VMEM((rows, rows), jnp.float32),
            dma((5,)),
            dma((chunks,)),
            dma((1,)),
            dma((2,)),
            dma((4, chunks)),
            dma((4, chunks)),
            dma((LEVELS, RADIX - 1)),
            dma((LEVELS, RADIX)),
        ],
        compiler_params=pltpu.CompilerParams(
            collective_id=0, has_side_effects=True, vmem_limit_bytes=48 * 1024 * 1024
        ),
    )(
        *(
            pltpu.with_memory_space_constraint(operand, pltpu.HBM)
            for operand in (
                data,
                primaries,
                wavelet,
                cover_ids.T,
                cover_counts.reshape(1, rows),
                waves,
            )
        )
    )
    return misfit, grad, series[0]


def solution(mesh):
    in_specs = (
        P("freq", None, "shot", None),
        P("freq", None, "shot", None),
        P("freq", None),
        P("shot", None),
        P("shot"),
    )
    out_specs = (P("freq", None, "shot", None), P("freq", None, "shot", None), P())
    return jax.shard_map(
        functools.partial(on_device, mesh.shape["shot"], mesh.shape["freq"]),
        mesh=mesh,
        in_specs=in_specs,
        out_specs=out_specs,
        check_vma=False,
    )
```

```python
import functools
import math

import jax
import jax.numpy as jnp
import numpy as np
from jax import lax
from jax.experimental import pallas as pl
from jax.experimental.pallas import tpu as pltpu
from jax.sharding import PartitionSpec as P

RB = 512
NT = 128
REACH = 2
PRE = 6
LAG = 5
BEHIND = 2
TAKE = 11
RADIX = 16
LEVELS = 2
MESH = pl.DeviceIdType.MESH


def kernel(
    dims,
    data,
    prim_hbm,
    wave_hbm,
    ids_hbm,
    counts_hbm,
    waves_hbm,
    misfit,
    grad,
    wavelet_grad,
    rec,
    own,
    near,
    mix,
    outer,
    window,
    sums,
    prim,
    wave,
    ids,
    counts,
    waves,
    cover,
    small_sem,
    own_sem,
    rec_sem,
    send_sem,
    recv_sem,
    sum_send_sem,
    sum_recv_sem,
):
    shots, freqs, chunks, rows = dims
    width = own.shape[3]
    tiles = width // rows
    me = lax.axis_index("shot")
    freq = lax.axis_index("freq")
    right = lax.rem(me + 1, shots)
    left = lax.rem(me + shots - 1, shots)

    def turn(first, count, step):
        later = step - count
        past = jnp.where(later < first, later, later + count)
        past = jnp.where(first + count > chunks, later + first + count - chunks, past)
        return jnp.where(step < count, lax.rem(first + step, chunks), past)

    def sent(block, step):
        first = lax.rem(lax.div(block, tiles) + chunks - 1, chunks)
        return turn(first, 3, step)

    def worked(step):
        return turn(lax.rem(lax.div(me + shots - REACH, tiles), chunks), 2, step)

    def load_own(chunk):
        columns = pl.ds(pl.multiple_of(chunk * width, width), width)
        return pltpu.make_async_copy(
            data.at[0, :, :, columns], own.at[chunk], own_sem.at[chunk]
        )

    load_rec = pltpu.make_async_copy(data.at[0], rec, rec_sem.at[0])

    inner = jnp.logical_and(me > 0, me < shots - 1)
    sends = (me < shots - 1, me > 0, inner, inner)
    takes = (me > 0, me < shots - 1, me > 1, me < shots - 2)

    def hop(stream, chunk):
        src = own.at[chunk] if stream < 2 else near.at[stream - 2, chunk]
        target = right if stream % 2 == 0 else left
        return pltpu.make_async_remote_copy(
            src_ref=src,
            dst_ref=near.at[stream, chunk],
            send_sem=send_sem.at[stream, chunk],
            recv_sem=recv_sem.at[stream, chunk],
            device_id=(target, freq),
            device_id_type=MESH,
        )

    line = RADIX // 2
    digits = [
        lax.rem(freq, 2) * line + lax.rem(me, line),
        lax.div(freq, 2) * line + lax.div(me, line),
    ]

    def partner(level, digit):
        first, second = lax.rem(digit, line), lax.div(digit, line)
        if level == 0:
            return (me - lax.rem(me, line) + first, freq - lax.rem(freq, 2) + second)
        return (first * line + lax.rem(me, line), second * 2 + lax.rem(freq, 2))

    def exchange(level, step):
        digit = lax.rem(digits[level] + step, RADIX)
        return pltpu.make_async_remote_copy(
            src_ref=sums.at[level, digits[level]],
            dst_ref=sums.at[level, digits[level]],
            send_sem=sum_send_sem.at[level, step - 1],
            recv_sem=sum_recv_sem.at[level, digits[level]],
            device_id=partner(level, digit),
            device_id_type=MESH,
        )

    def arrival(level, step):
        digit = lax.rem(digits[level] + step, RADIX)
        return pltpu.make_async_remote_copy(
            src_ref=sums.at[level, digit],
            dst_ref=sums.at[level, digit],
            send_sem=sum_send_sem.at[level, step - 1],
            recv_sem=sum_recv_sem.at[level, digit],
            device_id=partner(level, digit),
            device_id_type=MESH,
        )

    def sum_send(level, value):
        sums[level, digits[level]] = value
        for step in range(1, RADIX):
            exchange(level, step).start()

    def sum_take(level):
        for step in range(1, RADIX):
            arrival(level, step).wait_recv()
        total = sums[level, 0]
        for digit in range(1, RADIX):
            total = total + sums[level, digit]
        return total

    for step in range(chunks):
        load_own(sent(me, step)).start()
    small = [
        pltpu.make_async_copy(source, target, small_sem.at[spot])
        for spot, (source, target) in enumerate(
            [
                (wave_hbm, wave),
                (prim_hbm, prim),
                (ids_hbm, ids),
                (counts_hbm, counts),
                (waves_hbm, waves),
            ]
        )
    ]
    for copy in small:
        copy.start()
    load_rec.start()

    barrier = pltpu.get_barrier_semaphore()
    for target, there in ((left, sends[1]), (right, sends[0])):

        @pl.when(there)
        def _(target=target):
            pl.semaphore_signal(barrier, inc=1, device_id=(target, freq), device_id_type=MESH)

    for level in range(LEVELS):
        for step in range(1, RADIX):
            pl.semaphore_signal(
                barrier,
                inc=1,
                device_id=partner(level, lax.rem(digits[level] + step, RADIX)),
                device_id_type=MESH,
            )
    pl.semaphore_wait(barrier, jnp.where(inner, 2, 1) + LEVELS * (RADIX - 1))

    small[0].wait()
    diagonal = lax.broadcasted_iota(jnp.int32, (rows, rows), 0) == lax.broadcasted_iota(
        jnp.int32, (rows, rows), 1
    )
    for step in range(PRE):
        chunk = sent(me, step)
        load_own(chunk).wait()
        if step == 1:
            spot = pl.ds(pl.multiple_of(lax.rem(me, tiles) * rows, rows), rows)
            for part in range(2):
                tile = own[chunk, part, :, spot]
                moved = (tile.astype(jnp.float32) - wave[pl.ds(0, 1), pl.ds(part, 1)]).astype(jnp.bfloat16)
                own[chunk, part, :, spot] = jnp.where(diagonal, moved, tile)
        for stream in range(2):
            pl.when(sends[stream])(hop(stream, chunk).start)

    for copy in small[1:]:
        copy.wait()
    entry = lax.broadcasted_iota(jnp.int32, ids.shape, 0)
    listed = entry < counts[...]
    cover[...] = jnp.zeros_like(cover)
    for chunk in range(chunks):
        hit = jnp.logical_and(ids[...] == chunk, listed)
        cover[pl.ds(chunk, 1), :] = jnp.sum(jnp.where(hit, 1.0, 0.0), axis=0, keepdims=True)
    cover[...] = cover[...].T

    def inside(block):
        there = me + block - REACH
        return jnp.where(jnp.logical_and(there >= 0, there < shots), 1.0, 0.0)

    def response(part, block):
        tile = prim[0, part, :, pl.ds(block * rows, rows)]
        return tile.astype(jnp.float32) * inside(block)

    for block in range(2 * REACH + 1):
        real = response(0, block)
        imag = response(1, block)
        mix[block, pl.ds(0, rows), pl.ds(0, rows)] = real.astype(jnp.bfloat16)
        mix[block, pl.ds(0, rows), pl.ds(rows, rows)] = (-imag).astype(jnp.bfloat16)
        mix[block, pl.ds(rows, rows), pl.ds(0, rows)] = imag.astype(jnp.bfloat16)
        mix[block, pl.ds(rows, rows), pl.ds(rows, rows)] = real.astype(jnp.bfloat16)
    outer[...] = jnp.zeros_like(outer)
    for stream in range(4):

        @pl.when(jnp.logical_not(takes[stream]))
        def _(stream=stream):
            def clear(chunk, carry):
                near[stream, chunk] = jnp.zeros(near.shape[2:], near.dtype)
                return carry

            lax.fori_loop(0, chunks, clear, 0)

    load_rec.wait()

    def rows_of(block, chunk):
        ref = own.at[chunk] if block == REACH else near.at[(2, 0, -1, 1, 3)[block], chunk]
        return ref[...].reshape(2 * rows, width)

    def work(step):
        chunk = worked(step)
        for stream in (2, 3):
            pl.when(takes[stream])(hop(stream, chunk).wait_recv)
        columns = pl.ds(pl.multiple_of(chunk * width, width), width)
        predicted = jnp.dot(mix[0], rows_of(0, chunk), preferred_element_type=jnp.float32)
        for block in range(1, 2 * REACH + 1):
            predicted += jnp.dot(
                mix[block], rows_of(block, chunk), preferred_element_type=jnp.float32
            )
        lane = lax.broadcasted_iota(jnp.int32, cover.shape, 1)
        mask = jnp.sum(jnp.where(lane == chunk, cover[...], 0.0), axis=1, keepdims=True)
        record = rec[:, :, columns].astype(jnp.float32)
        residual = (mask[None] * (record + predicted.reshape(2, rows, width))).astype(
            jnp.bfloat16
        )

        misfit[0, :, :, columns] = residual

        @pl.when(step < 2)
        def _():
            window[:, :, pl.ds(pl.multiple_of(step * width, width), width)] = residual

        flat = residual.reshape(2 * rows, width)
        for block in range(2 * REACH + 1):
            outer[block] += lax.dot_general(
                flat,
                rows_of(block, chunk),
                (((1,), (1,)), ((), ())),
                preferred_element_type=jnp.float32,
            )

    def correlate():
        offset = lax.rem(me + shots - REACH, tiles) * rows
        real = jnp.zeros((rows, rows), jnp.float32)
        imag = jnp.zeros((rows, rows), jnp.float32)
        for block in range(2 * REACH + 1):
            spot = pl.ds(pl.multiple_of(offset + block * rows, rows), rows)
            resid_re = window[0, :, spot].astype(jnp.float32)
            resid_im = window[1, :, spot].astype(jnp.float32)
            resp_re = response(0, block)
            resp_im = response(1, block)
            real += resp_re * resid_re + resp_im * resid_im
            imag += resp_re * resid_im - resp_im * resid_re
        line = lax.broadcasted_iota(jnp.int32, waves.shape, 0)
        cosine = jnp.sum(jnp.where(line == freq, waves[...], 0.0), axis=0, keepdims=True)
        sine = jnp.sum(jnp.where(line == freq + freqs, waves[...], 0.0), axis=0, keepdims=True)
        series = jnp.sum(imag) * sine - jnp.sum(real) * cosine
        return jnp.broadcast_to(series, sums.shape[2:])

    def body(step, carry):
        @pl.when(step < chunks)
        def _():
            chunk = sent(left, step)
            pl.when(takes[0])(hop(0, chunk).wait_recv)
            pl.when(sends[2])(hop(2, chunk).start)
            chunk = sent(right, step)
            pl.when(takes[1])(hop(1, chunk).wait_recv)
            pl.when(sends[3])(hop(3, chunk).start)

        @pl.when(step < chunks - PRE)
        def _():
            chunk = sent(me, step + PRE)
            load_own(chunk).wait()
            for stream in range(2):
                pl.when(sends[stream])(hop(stream, chunk).start)

        @pl.when(step >= LAG)
        def _():
            work(step - LAG)
            chunk = sent(me, step - LAG)
            for stream in range(2):
                pl.when(sends[stream])(hop(stream, chunk).wait_send)

        @pl.when(step >= LAG + BEHIND)
        def _():
            past = step - LAG - BEHIND
            pl.when(sends[2])(hop(2, sent(left, past)).wait_send)
            pl.when(sends[3])(hop(3, sent(right, past)).wait_send)

        @pl.when(step == LAG + 1)
        def _():
            sum_send(0, correlate())

        @pl.when(step == TAKE)
        def _():
            sum_send(1, sum_take(0))

        @pl.when(step == chunks + LAG - 3)
        def _():
            scale = 1.0 / math.sqrt(shots * rows * rows * (2 * REACH + 1))
            wavelet_grad[...] = sum_take(1) * scale
            for level in range(LEVELS):
                for near_by in range(1, RADIX):
                    exchange(level, near_by).wait_send()

        return carry

    lax.fori_loop(0, chunks + LAG, body, 0)

    for block in range(2 * REACH + 1):
        spot = pl.ds(block * rows, rows)
        low, high = pl.ds(0, rows), pl.ds(rows, rows)
        real = outer[block, low, low] + outer[block, high, high]
        imag = outer[block, high, low] - outer[block, low, high]
        grad[0, 0, :, spot] = real * inside(block)
        grad[0, 1, :, spot] = imag * inside(block)

    for past in range(chunks - BEHIND, chunks):
        pl.when(sends[2])(hop(2, sent(left, past)).wait_send)
        pl.when(sends[3])(hop(3, sent(right, past)).wait_send)


def flush(misfit, grad, series, misfit_out, grad_out, series_out, sems):
    parts = [(series, series_out), (grad, grad_out)]
    for part in range(2):
        for spot in range(8):
            rows = pl.ds(spot * 16, 16)
            parts.append((misfit.at[0, part, rows], misfit_out.at[0, part, rows]))
    copies = [
        pltpu.make_async_copy(source, target, sems.at[spot])
        for spot, (source, target) in enumerate(parts)
    ]
    for copy in copies:
        copy.start()
    for copy in copies:
        copy.wait()


def on_device(shots, freqs, data, primaries, wavelet, cover_ids, cover_counts):
    _, _, rows, width = data.shape
    chunks = width // RB
    band = primaries.shape[3]
    times = np.arange(NT, dtype=np.float32)
    phase = np.stack(
        [np.float32(2.0 * math.pi * (f + 1)) * times / np.float32(NT) for f in range(freqs)]
    )
    waves = jnp.asarray(np.concatenate([np.cos(phase), np.sin(phase)]).astype(np.float32))
    vmem = pl.BlockSpec(memory_space=pltpu.VMEM)
    hbm = pl.BlockSpec(memory_space=pltpu.HBM)
    blocks = 2 * REACH + 1
    dma = pltpu.SemaphoreType.DMA
    misfit, grad, series = pl.pallas_call(
        functools.partial(kernel, (shots, freqs, chunks, rows)),
        out_shape=(
            jax.ShapeDtypeStruct(data.shape, jnp.bfloat16),
            jax.ShapeDtypeStruct((1, 2, rows, band), jnp.float32),
            jax.ShapeDtypeStruct((1, NT), jnp.float32),
        ),
        in_specs=[hbm] * 6,
        out_specs=(vmem, vmem, vmem),
        scratch_shapes=[
            pltpu.VMEM((2, rows, width), jnp.bfloat16),
            pltpu.VMEM((chunks, 2, rows, RB), jnp.bfloat16),
            pltpu.VMEM((4, chunks, 2, rows, RB), jnp.bfloat16),
            pltpu.VMEM((blocks, 2 * rows, 2 * rows), jnp.bfloat16),
            pltpu.VMEM((blocks, 2 * rows, 2 * rows), jnp.float32),
            pltpu.VMEM((2, rows, 2 * RB), jnp.bfloat16),
            pltpu.VMEM((LEVELS, RADIX, 1, NT), jnp.float32),
            pltpu.VMEM(primaries.shape, jnp.bfloat16),
            pltpu.VMEM(wavelet.shape, jnp.float32),
            pltpu.VMEM(cover_ids.shape[::-1], jnp.int32),
            pltpu.VMEM((1, rows), jnp.int32),
            pltpu.VMEM(waves.shape, jnp.float32),
            pltpu.VMEM((rows, rows), jnp.float32),
            dma((5,)),
            dma((chunks,)),
            dma((1,)),
            dma((4, chunks)),
            dma((4, chunks)),
            dma((LEVELS, RADIX - 1)),
            dma((LEVELS, RADIX)),
        ],
        compiler_params=pltpu.CompilerParams(
            collective_id=0, has_side_effects=True, vmem_limit_bytes=48 * 1024 * 1024
        ),
    )(
        *(
            pltpu.with_memory_space_constraint(operand, pltpu.HBM)
            for operand in (
                data,
                primaries,
                wavelet,
                cover_ids.T,
                cover_counts.reshape(1, rows),
                waves,
            )
        )
    )
    results = (misfit, grad, series)
    misfit, grad, series = pl.pallas_call(
        flush,
        out_shape=tuple(pltpu.HBM(part.shape, part.dtype) for part in results),
        in_specs=[vmem] * 3,
        out_specs=(hbm,) * 3,
        scratch_shapes=[dma((18,))],
        compiler_params=pltpu.CompilerParams(vmem_limit_bytes=8 * 1024 * 1024),
    )(*(pltpu.with_memory_space_constraint(part, pltpu.VMEM) for part in results))
    return misfit, grad, series[0]


def solution(mesh):
    in_specs = (
        P("freq", None, "shot", None),
        P("freq", None, "shot", None),
        P("freq", None),
        P("shot", None),
        P("shot"),
    )
    out_specs = (P("freq", None, "shot", None), P("freq", None, "shot", None), P())
    return jax.shard_map(
        functools.partial(on_device, mesh.shape["shot"], mesh.shape["freq"]),
        mesh=mesh,
        in_specs=in_specs,
        out_specs=out_specs,
        check_vma=False,
    )
```

```python
import functools
import math

import jax
import jax.numpy as jnp
import numpy as np
from jax import lax
from jax.experimental import pallas as pl
from jax.experimental.pallas import tpu as pltpu
from jax.sharding import PartitionSpec as P

RB = 512
NT = 128
REACH = 2
PRE = 6
LAG = 5
BEHIND = 2
TAKE = 11
RADIX = 16
LEVELS = 2
MESH = pl.DeviceIdType.MESH


def kernel(
    dims,
    data,
    prim_hbm,
    wave_hbm,
    ids_hbm,
    counts_hbm,
    waves_hbm,
    misfit,
    grad,
    wavelet_grad,
    rec,
    near,
    mix,
    outer,
    window,
    sums,
    prim,
    wave,
    ids,
    counts,
    waves,
    cover,
    small_sem,
    own_sem,
    rec_sem,
    send_sem,
    recv_sem,
    sum_send_sem,
    sum_recv_sem,
):
    shots, freqs, chunks, rows = dims
    width = near.shape[4]
    place = (1, 3, 0, 4)
    band = 2 * REACH + 1
    tiles = width // rows
    me = lax.axis_index("shot")
    freq = lax.axis_index("freq")
    right = lax.rem(me + 1, shots)
    left = lax.rem(me + shots - 1, shots)

    def turn(first, count, step):
        later = step - count
        past = jnp.where(later < first, later, later + count)
        past = jnp.where(first + count > chunks, later + first + count - chunks, past)
        return jnp.where(step < count, lax.rem(first + step, chunks), past)

    def sent(block, step):
        first = lax.rem(lax.div(block, tiles) + chunks - 1, chunks)
        return turn(first, 3, step)

    def worked(step):
        return turn(lax.rem(lax.div(me + shots - REACH, tiles), chunks), 2, step)

    def load_own(chunk):
        columns = pl.ds(pl.multiple_of(chunk * width, width), width)
        return pltpu.make_async_copy(
            data.at[0, :, :, columns], near.at[chunk, REACH], own_sem.at[chunk]
        )

    load_rec = pltpu.make_async_copy(data.at[0], rec, rec_sem.at[0])

    inner = jnp.logical_and(me > 0, me < shots - 1)
    sends = (me < shots - 1, me > 0, inner, inner)
    takes = (me > 0, me < shots - 1, me > 1, me < shots - 2)

    def hop(stream, chunk):
        src = near.at[chunk, REACH if stream < 2 else place[stream - 2]]
        target = right if stream % 2 == 0 else left
        return pltpu.make_async_remote_copy(
            src_ref=src,
            dst_ref=near.at[chunk, place[stream]],
            send_sem=send_sem.at[stream, chunk],
            recv_sem=recv_sem.at[stream, chunk],
            device_id=(target, freq),
            device_id_type=MESH,
        )

    line = RADIX // 2
    digits = [
        lax.rem(freq, 2) * line + lax.rem(me, line),
        lax.div(freq, 2) * line + lax.div(me, line),
    ]

    def partner(level, digit):
        first, second = lax.rem(digit, line), lax.div(digit, line)
        if level == 0:
            return (me - lax.rem(me, line) + first, freq - lax.rem(freq, 2) + second)
        return (first * line + lax.rem(me, line), second * 2 + lax.rem(freq, 2))

    def exchange(level, step):
        digit = lax.rem(digits[level] + step, RADIX)
        return pltpu.make_async_remote_copy(
            src_ref=sums.at[level, digits[level]],
            dst_ref=sums.at[level, digits[level]],
            send_sem=sum_send_sem.at[level, step - 1],
            recv_sem=sum_recv_sem.at[level, digits[level]],
            device_id=partner(level, digit),
            device_id_type=MESH,
        )

    def arrival(level, step):
        digit = lax.rem(digits[level] + step, RADIX)
        return pltpu.make_async_remote_copy(
            src_ref=sums.at[level, digit],
            dst_ref=sums.at[level, digit],
            send_sem=sum_send_sem.at[level, step - 1],
            recv_sem=sum_recv_sem.at[level, digit],
            device_id=partner(level, digit),
            device_id_type=MESH,
        )

    def sum_send(level, value):
        sums[level, digits[level]] = value
        for step in range(1, RADIX):
            exchange(level, step).start()

    def sum_take(level):
        for step in range(1, RADIX):
            arrival(level, step).wait_recv()
        total = sums[level, 0]
        for digit in range(1, RADIX):
            total = total + sums[level, digit]
        return total

    small = [
        pltpu.make_async_copy(source, target, small_sem.at[spot])
        for spot, (source, target) in enumerate(
            [
                (wave_hbm, wave),
                (prim_hbm, prim),
                (ids_hbm, ids),
                (counts_hbm, counts),
                (waves_hbm, waves),
            ]
        )
    ]
    small[0].start()
    for step in range(PRE):
        load_own(sent(me, step)).start()
    for copy in small[1:]:
        copy.start()

    barrier = pltpu.get_barrier_semaphore()
    for target, there in ((left, sends[1]), (right, sends[0])):

        @pl.when(there)
        def _(target=target):
            pl.semaphore_signal(barrier, inc=1, device_id=(target, freq), device_id_type=MESH)

    for level in range(LEVELS):
        for step in range(1, RADIX):
            pl.semaphore_signal(
                barrier,
                inc=1,
                device_id=partner(level, lax.rem(digits[level] + step, RADIX)),
                device_id_type=MESH,
            )
    pl.semaphore_wait(barrier, jnp.where(inner, 2, 1) + LEVELS * (RADIX - 1))

    diagonal = lax.broadcasted_iota(jnp.int32, (rows, rows), 0) == lax.broadcasted_iota(
        jnp.int32, (rows, rows), 1
    )
    for step in range(PRE):
        chunk = sent(me, step)
        load_own(chunk).wait()
        if step == 1:
            small[0].wait()
            spot = pl.ds(pl.multiple_of(lax.rem(me, tiles) * rows, rows), rows)
            for part in range(2):
                tile = near[chunk, REACH, part, :, spot]
                moved = (tile.astype(jnp.float32) - wave[pl.ds(0, 1), pl.ds(part, 1)]).astype(jnp.bfloat16)
                near[chunk, REACH, part, :, spot] = jnp.where(diagonal, moved, tile)
        for stream in range(2):
            pl.when(sends[stream])(hop(stream, chunk).start)

    for step in range(PRE, chunks):
        load_own(sent(me, step)).start()
    load_rec.start()
    for copy in small[1:]:
        copy.wait()
    entry = lax.broadcasted_iota(jnp.int32, ids.shape, 0)
    listed = entry < counts[...]
    cover[...] = jnp.zeros_like(cover)
    for chunk in range(chunks):
        hit = jnp.logical_and(ids[...] == chunk, listed)
        cover[pl.ds(chunk, 1), :] = jnp.sum(jnp.where(hit, 1.0, 0.0), axis=0, keepdims=True)
    cover[...] = cover[...].T

    def inside(block):
        there = me + block - REACH
        return jnp.where(jnp.logical_and(there >= 0, there < shots), 1.0, 0.0)

    def response(part, block):
        tile = prim[0, part, :, pl.ds(block * rows, rows)]
        return tile.astype(jnp.float32) * inside(block)

    for block in range(2 * REACH + 1):
        real = response(0, block)
        imag = response(1, block)
        upper, lower = pl.ds(0, rows), pl.ds(rows, rows)
        first, second = pl.ds(2 * block * rows, rows), pl.ds((2 * block + 1) * rows, rows)
        mix[upper, first] = real.astype(jnp.bfloat16)
        mix[upper, second] = (-imag).astype(jnp.bfloat16)
        mix[lower, first] = imag.astype(jnp.bfloat16)
        mix[lower, second] = real.astype(jnp.bfloat16)
    outer[...] = jnp.zeros_like(outer)
    for stream in range(4):

        @pl.when(jnp.logical_not(takes[stream]))
        def _(stream=stream):
            def clear(chunk, carry):
                near[chunk, place[stream]] = jnp.zeros(near.shape[2:], near.dtype)
                return carry

            lax.fori_loop(0, chunks, clear, 0)

    load_rec.wait()

    def work(step):
        chunk = worked(step)
        for stream in (2, 3):
            pl.when(takes[stream])(hop(stream, chunk).wait_recv)
        columns = pl.ds(pl.multiple_of(chunk * width, width), width)
        nearby = near[chunk].reshape(2 * band * rows, width)
        predicted = jnp.dot(mix[...], nearby, preferred_element_type=jnp.float32)
        lane = lax.broadcasted_iota(jnp.int32, cover.shape, 1)
        mask = jnp.sum(jnp.where(lane == chunk, cover[...], 0.0), axis=1, keepdims=True)
        record = rec[:, :, columns].astype(jnp.float32)
        residual = (mask[None] * (record + predicted.reshape(2, rows, width))).astype(
            jnp.bfloat16
        )

        misfit[0, :, :, columns] = residual

        @pl.when(step < 2)
        def _():
            window[:, :, pl.ds(pl.multiple_of(step * width, width), width)] = residual

        outer[...] += lax.dot_general(
            residual.reshape(2 * rows, width),
            nearby,
            (((1,), (1,)), ((), ())),
            preferred_element_type=jnp.float32,
        )

    def correlate():
        offset = lax.rem(me + shots - REACH, tiles) * rows
        real = jnp.zeros((rows, rows), jnp.float32)
        imag = jnp.zeros((rows, rows), jnp.float32)
        for block in range(2 * REACH + 1):
            spot = pl.ds(pl.multiple_of(offset + block * rows, rows), rows)
            resid_re = window[0, :, spot].astype(jnp.float32)
            resid_im = window[1, :, spot].astype(jnp.float32)
            resp_re = response(0, block)
            resp_im = response(1, block)
            real += resp_re * resid_re + resp_im * resid_im
            imag += resp_re * resid_im - resp_im * resid_re
        line = lax.broadcasted_iota(jnp.int32, waves.shape, 0)
        cosine = jnp.sum(jnp.where(line == freq, waves[...], 0.0), axis=0, keepdims=True)
        sine = jnp.sum(jnp.where(line == freq + freqs, waves[...], 0.0), axis=0, keepdims=True)
        series = jnp.sum(imag) * sine - jnp.sum(real) * cosine
        return jnp.broadcast_to(series, sums.shape[2:])

    def body(step, carry):
        @pl.when(step < chunks)
        def _():
            chunk = sent(left, step)
            pl.when(takes[0])(hop(0, chunk).wait_recv)
            pl.when(sends[2])(hop(2, chunk).start)
            chunk = sent(right, step)
            pl.when(takes[1])(hop(1, chunk).wait_recv)
            pl.when(sends[3])(hop(3, chunk).start)

        @pl.when(step < chunks - PRE)
        def _():
            chunk = sent(me, step + PRE)
            load_own(chunk).wait()
            for stream in range(2):
                pl.when(sends[stream])(hop(stream, chunk).start)

        @pl.when(step >= LAG)
        def _():
            work(step - LAG)
            chunk = sent(me, step - LAG)
            for stream in range(2):
                pl.when(sends[stream])(hop(stream, chunk).wait_send)

        @pl.when(step >= LAG + BEHIND)
        def _():
            past = step - LAG - BEHIND
            pl.when(sends[2])(hop(2, sent(left, past)).wait_send)
            pl.when(sends[3])(hop(3, sent(right, past)).wait_send)

        @pl.when(step == LAG + 1)
        def _():
            sum_send(0, correlate())

        @pl.when(step == TAKE)
        def _():
            sum_send(1, sum_take(0))

        @pl.when(step == chunks + LAG - 3)
        def _():
            scale = 1.0 / math.sqrt(shots * rows * rows * (2 * REACH + 1))
            wavelet_grad[...] = sum_take(1) * scale
            for level in range(LEVELS):
                for near_by in range(1, RADIX):
                    exchange(level, near_by).wait_send()

        return carry

    lax.fori_loop(0, chunks + LAG, body, 0)

    for block in range(2 * REACH + 1):
        spot = pl.ds(block * rows, rows)
        upper, lower = pl.ds(0, rows), pl.ds(rows, rows)
        first, second = pl.ds(2 * block * rows, rows), pl.ds((2 * block + 1) * rows, rows)
        real = outer[upper, first] + outer[lower, second]
        imag = outer[lower, first] - outer[upper, second]
        grad[0, 0, :, spot] = real * inside(block)
        grad[0, 1, :, spot] = imag * inside(block)

    for past in range(chunks - BEHIND, chunks):
        pl.when(sends[2])(hop(2, sent(left, past)).wait_send)
        pl.when(sends[3])(hop(3, sent(right, past)).wait_send)


def flush(misfit, grad, series, misfit_out, grad_out, series_out, sems):
    parts = [(series, series_out), (grad, grad_out)]
    for part in range(2):
        for spot in range(8):
            rows = pl.ds(spot * 16, 16)
            parts.append((misfit.at[0, part, rows], misfit_out.at[0, part, rows]))
    copies = [
        pltpu.make_async_copy(source, target, sems.at[spot])
        for spot, (source, target) in enumerate(parts)
    ]
    for copy in copies:
        copy.start()
    for copy in copies:
        copy.wait()


def on_device(shots, freqs, data, primaries, wavelet, cover_ids, cover_counts):
    _, _, rows, width = data.shape
    chunks = width // RB
    band = primaries.shape[3]
    times = np.arange(NT, dtype=np.float32)
    phase = np.stack(
        [np.float32(2.0 * math.pi * (f + 1)) * times / np.float32(NT) for f in range(freqs)]
    )
    waves = jnp.asarray(np.concatenate([np.cos(phase), np.sin(phase)]).astype(np.float32))
    vmem = pl.BlockSpec(memory_space=pltpu.VMEM)
    hbm = pl.BlockSpec(memory_space=pltpu.HBM)
    blocks = 2 * REACH + 1
    dma = pltpu.SemaphoreType.DMA
    misfit, grad, series = pl.pallas_call(
        functools.partial(kernel, (shots, freqs, chunks, rows)),
        out_shape=(
            jax.ShapeDtypeStruct(data.shape, jnp.bfloat16),
            jax.ShapeDtypeStruct((1, 2, rows, band), jnp.float32),
            jax.ShapeDtypeStruct((1, NT), jnp.float32),
        ),
        in_specs=[hbm] * 6,
        out_specs=(vmem, vmem, vmem),
        scratch_shapes=[
            pltpu.VMEM((2, rows, width), jnp.bfloat16),
            pltpu.VMEM((chunks, blocks, 2, rows, RB), jnp.bfloat16),
            pltpu.VMEM((2 * rows, 2 * band), jnp.bfloat16),
            pltpu.VMEM((2 * rows, 2 * band), jnp.float32),
            pltpu.VMEM((2, rows, 2 * RB), jnp.bfloat16),
            pltpu.VMEM((LEVELS, RADIX, 1, NT), jnp.float32),
            pltpu.VMEM(primaries.shape, jnp.bfloat16),
            pltpu.VMEM(wavelet.shape, jnp.float32),
            pltpu.VMEM(cover_ids.shape[::-1], jnp.int32),
            pltpu.VMEM((1, rows), jnp.int32),
            pltpu.VMEM(waves.shape, jnp.float32),
            pltpu.VMEM((rows, rows), jnp.float32),
            dma((5,)),
            dma((chunks,)),
            dma((1,)),
            dma((4, chunks)),
            dma((4, chunks)),
            dma((LEVELS, RADIX - 1)),
            dma((LEVELS, RADIX)),
        ],
        compiler_params=pltpu.CompilerParams(
            collective_id=0, has_side_effects=True, vmem_limit_bytes=48 * 1024 * 1024
        ),
    )(
        *(
            pltpu.with_memory_space_constraint(operand, pltpu.HBM)
            for operand in (
                data,
                primaries,
                wavelet,
                cover_ids.T,
                cover_counts.reshape(1, rows),
                waves,
            )
        )
    )
    results = (misfit, grad, series)
    misfit, grad, series = pl.pallas_call(
        flush,
        out_shape=tuple(pltpu.HBM(part.shape, part.dtype) for part in results),
        in_specs=[vmem] * 3,
        out_specs=(hbm,) * 3,
        scratch_shapes=[dma((18,))],
        compiler_params=pltpu.CompilerParams(vmem_limit_bytes=8 * 1024 * 1024),
    )(*(pltpu.with_memory_space_constraint(part, pltpu.VMEM) for part in results))
    return misfit, grad, series[0]


def solution(mesh):
    in_specs = (
        P("freq", None, "shot", None),
        P("freq", None, "shot", None),
        P("freq", None),
        P("shot", None),
        P("shot"),
    )
    out_specs = (P("freq", None, "shot", None), P("freq", None, "shot", None), P())
    return jax.shard_map(
        functools.partial(on_device, mesh.shape["shot"], mesh.shape["freq"]),
        mesh=mesh,
        in_specs=in_specs,
        out_specs=out_specs,
        check_vma=False,
    )
```
